32 devices in a mesh: seq: 4 (over x, core), fsdp: 8 (over z, y).
Axes of the slice: x: 2, y: 2, z: 4, core: 2. Of those that a mesh axis runs over, the one named last changes fastest.
Arguments:
- tokens: bfloat16 [2, 16, 128, 768], P(None, 'fsdp', 'seq'), may hold values from -6 to 6
- cotangent: bfloat16 [2, 16, 128, 768], P(None, 'fsdp', 'seq'), may hold values from -6 to 6
- span_order: int32 [2, 16], replicated, may hold values from 0 to 15, each once within a row
- ln1_gain: bfloat16 [768], P('fsdp'), may hold values from 0.5 to 1.5
- ln1_bias: bfloat16 [768], P('fsdp'), may hold values from -1.5 to 1.5
- w_qkv: bfloat16 [768, 2304], P('fsdp'), may hold values from -0.21875 to 0.21875
- bias_query: bfloat16 [768], P('fsdp'), may hold values from -1.5 to 1.5
- bias_value: bfloat16 [768], P('fsdp'), may hold values from -1.5 to 1.5
- w_out: bfloat16 [768, 768], P('fsdp'), may hold values from -0.3125 to 0.3125
- bias_out: bfloat16 [768], P('fsdp'), may hold values from -1.5 to 1.5
- ln2_gain: bfloat16 [768], P('fsdp'), may hold values from 0.5 to 1.5
- ln2_bias: bfloat16 [768], P('fsdp'), may hold values from -1.5 to 1.5
- w_fc: bfloat16 [768, 3072], P('fsdp'), may hold values from -0.21875 to 0.21875
- bias_fc: bfloat16 [3072], P('fsdp'), may hold values from -1.5 to 1.5
- w_proj: bfloat16 [3072, 768], P('fsdp'), may hold values from -0.109375 to 0.109375
- bias_proj: bfloat16 [768], P('fsdp'), may hold values from -1.5 to 1.5
Outputs:
- layer_out: float32 [2, 16, 128, 768], P(None, 'fsdp', 'seq')
- input_grad: float32 [2, 16, 128, 768], P(None, 'fsdp', 'seq')
- grad_ln1_gain: float32 [768], P('fsdp')
- grad_ln1_bias: float32 [768], P('fsdp')
- grad_qkv: float32 [768, 2304], P('fsdp')
- grad_bias_query: float32 [768], P('fsdp')
- grad_bias_value: float32 [768], P('fsdp')
- grad_out: float32 [768, 768], P('fsdp')
- grad_bias_out: float32 [768], P('fsdp')
- grad_ln2_gain: float32 [768], P('fsdp')
- grad_ln2_bias: float32 [768], P('fsdp')
- grad_fc: float32 [768, 3072], P('fsdp')
- grad_bias_fc: float32 [3072], P('fsdp')
- grad_proj: float32 [3072, 768], P('fsdp')
- grad_bias_proj: float32 [768], P('fsdp')
The draws below stay inside these ranges and needn't reach their ends.
Inputs may be any that keep to these rules, and one draw needn't show every extreme that they name: Each row names every one of the 16 blocks of a sequence once; slot c of sequence s holds the positions span_order[s, c] * 128 to span_order[s, c] * 128 + 127 in order.
All inputs are finite; a program needn't handle non-finite values.
Results may differ from the reference program's by a relative error of at most 0.03.
Values may be sent and summed in bfloat16 or wider, within the bound.
No kernel may reach another device: no remote copies, remote signals or barrier semaphores. Data moves between devices by JAX's collectives and lax.ppermute only.
A program may use at most 192 MiB of HBM per device.

```python
import math
import jax
import jax.numpy as jnp
from jax import lax

D = 768
HEADS = 12
HEAD_DIM = 64
FF = 3072
SEQS = 2
SPAN = 128
SPANS = 16
SEQ_LEN = 2048


def levels(stream_key, shape, cuts, least, top_value):
    def one(position, shards_of):
        draws = jax.random.uniform(jax.random.fold_in(jax.random.fold_in(stream_key, 6), position), (shards_of,), jnp.float32, least / len(cuts), top_value / len(cuts))
        return jnp.repeat(jnp.exp(draws), shape[position] // shards_of).reshape((-1,) + (1,) * (len(shape) - position - 1))

    factor_of = one(*cuts[0])
    for cut in cuts[1:]:
        factor_of = factor_of * one(*cut)
    return factor_of


def bell_draw(stream_key, shape, scale, limit, shards=(), kind=jnp.bfloat16):
    loudness = levels(stream_key, shape, shards, -0.22, 0.18) if shards else 1.0
    values = jax.random.normal(stream_key, shape, jnp.float32) * scale * loudness
    return jnp.minimum(jnp.maximum(values, -limit), limit).astype(kind)


def setup_inputs(seed: int = 0) -> dict:
    arg_keys = jax.random.split(jax.random.key(seed), 17)
    tokens = bell_draw(arg_keys[0], (SEQS, SPANS, SPAN, D), 1.0, 6.0, ((1, 8), (2, 4)))
    cotangent = bell_draw(arg_keys[1], (SEQS, SPANS, SPAN, D), 1.0, 6.0, ((1, 8), (2, 4)))
    span_order = jax.vmap(lambda own: jax.random.permutation(own, SPANS))(jax.random.split(arg_keys[2], SEQS)).reshape((SEQS, SPANS)).astype(jnp.int32)
    ln1_gain = jnp.clip(1.0 + 0.1 * jax.random.normal(arg_keys[3], (D,), jnp.float32), 0.5, 1.5).astype(jnp.bfloat16)
    ln1_bias = bell_draw(arg_keys[4], (D,), 0.3, 1.5, ((0, 8),))
    w_qkv = bell_draw(arg_keys[5], (D, 3 * D), D ** -0.5, 0.21875, ((0, 8),))
    bias_query = bell_draw(arg_keys[6], (D,), 0.3, 1.5, ((0, 8),))
    bias_value = bell_draw(arg_keys[7], (D,), 0.3, 1.5, ((0, 8),))
    w_out = bell_draw(arg_keys[8], (D, D), (D // 2) ** -0.5, 0.3125, ((0, 8),))
    bias_out = bell_draw(arg_keys[9], (D,), 0.3, 1.5, ((0, 8),))
    ln2_gain = jnp.clip(1.0 + 0.1 * jax.random.normal(arg_keys[10], (D,), jnp.float32), 0.5, 1.5).astype(jnp.bfloat16)
    ln2_bias = bell_draw(arg_keys[11], (D,), 0.3, 1.5, ((0, 8),))
    w_fc = bell_draw(arg_keys[12], (D, FF), D ** -0.5, 0.21875, ((0, 8),))
    bias_fc = bell_draw(arg_keys[13], (FF,), 0.3, 1.5, ((0, 8),))
    w_proj = bell_draw(arg_keys[14], (FF, D), FF ** -0.5, 0.109375, ((0, 8),))
    bias_proj = bell_draw(arg_keys[15], (D,), 0.3, 1.5, ((0, 8),))
    return dict(tokens=tokens, cotangent=cotangent, span_order=span_order, ln1_gain=ln1_gain, ln1_bias=ln1_bias, w_qkv=w_qkv, bias_query=bias_query, bias_value=bias_value, w_out=w_out, bias_out=bias_out, ln2_gain=ln2_gain, ln2_bias=ln2_bias, w_fc=w_fc, bias_fc=bias_fc, w_proj=w_proj, bias_proj=bias_proj)


@jax.custom_vjp
def low(v):
    return lax.optimization_barrier(v.astype(jnp.bfloat16)).astype(jnp.float32)

@jax.custom_vjp
def low_back(v):
    return v

def low_keep(v):
    return (low(v), None)

def low_pass(kept, grad):
    return (grad,)

def back_keep(v):
    return (v, None)

def back_low(kept, grad):
    return (low(grad),)
low.defvjp(low_keep, low_pass)
low_back.defvjp(back_keep, back_low)
EPSILON = 1e-05
NEGATIVE = -1e+30
HIGHEST = lax.Precision.HIGHEST

def norm_rows(token_rows, scale_gain, offset):
    average = lax.optimization_barrier(jnp.mean(token_rows, axis=-1, keepdims=True))
    centered = token_rows - average
    variance = lax.optimization_barrier(jnp.mean(centered * centered, axis=-1, keepdims=True))
    return centered * lax.rsqrt(variance + EPSILON) * scale_gain + offset

def product(left_side, right_side):
    return jnp.dot(left_side, right_side, precision=HIGHEST, preferred_element_type=jnp.float32)

def attend_sequence(queries, key_part, value_part, positions):
    length = queries.shape[0]
    block_rows = math.gcd(length, 512)
    query_blocks = queries.reshape(length // block_rows, block_rows, HEADS, HEAD_DIM)
    position_blocks = positions.reshape(length // block_rows, block_rows)

    def one_block(block_pair):
        query_block, query_pos = block_pair
        scores = low_back(jnp.einsum('qhe,khe->hqk', query_block, key_part, precision=HIGHEST) * 0.125)
        allowed = query_pos[:, None] >= positions[None, :]
        scores = jnp.where(allowed[None], scores, NEGATIVE)
        probs = low(jax.nn.softmax(scores, axis=-1))
        return jnp.einsum('hqk,khe->qhe', probs, value_part, precision=HIGHEST)
    outputs = lax.map(jax.checkpoint(one_block), (query_blocks, position_blocks))
    return outputs.reshape(length, HEADS, HEAD_DIM)

def reference(tokens, cotangent, span_order, ln1_gain, ln1_bias, w_qkv, bias_query, bias_value, w_out, bias_out, ln2_gain, ln2_bias, w_fc, bias_fc, w_proj, bias_proj):
    offsets = jnp.arange(SPAN, dtype=jnp.int32)
    positions = (span_order[:, :, None] * SPAN + offsets[None, None, :]).reshape(SEQS, SEQ_LEN)

    def layer(token_in, gain_one, offset_one, qkv_weight, query_bias, value_bias, out_weight, out_bias, gain_two, offset_two, fc_weight, fc_bias, proj_weight, proj_bias):
        token_rows = token_in.reshape(SEQS, SEQ_LEN, D)
        normed_one = low(norm_rows(token_rows, gain_one, offset_one))
        qkv_bias = jnp.concatenate([query_bias, jnp.zeros_like(query_bias), value_bias])
        projected = low(low_back(product(normed_one, qkv_weight) + qkv_bias))
        queries = projected[..., :D].reshape(SEQS, SEQ_LEN, HEADS, HEAD_DIM)
        key_part = projected[..., D:2 * D].reshape(SEQS, SEQ_LEN, HEADS, HEAD_DIM)
        value_part = projected[..., 2 * D:].reshape(SEQS, SEQ_LEN, HEADS, HEAD_DIM)
        attended = jnp.stack([attend_sequence(queries[number], key_part[number], value_part[number], positions[number]) for number in range(SEQS)])
        attended = low(low_back(attended.reshape(SEQS, SEQ_LEN, D)))
        attn_out = low_back(product(attended, out_weight) + out_bias)
        residual = token_rows + attn_out
        normed_two = low(norm_rows(residual, gain_two, offset_two))
        hidden_pre = low_back(product(normed_two, fc_weight) + fc_bias)
        activated = low(jax.nn.gelu(hidden_pre, approximate=True))
        result = residual + product(activated, proj_weight) + proj_bias
        return result.reshape(token_in.shape)
    floats = (tokens.astype(jnp.float32), ln1_gain.astype(jnp.float32), ln1_bias.astype(jnp.float32), w_qkv.astype(jnp.float32), bias_query.astype(jnp.float32), bias_value.astype(jnp.float32), w_out.astype(jnp.float32), bias_out.astype(jnp.float32), ln2_gain.astype(jnp.float32), ln2_bias.astype(jnp.float32), w_fc.astype(jnp.float32), bias_fc.astype(jnp.float32), w_proj.astype(jnp.float32), bias_proj.astype(jnp.float32))
    layer_out, pullback = jax.vjp(layer, *floats)
    grads = pullback(cotangent.astype(jnp.float32))
    return (layer_out, grads[0], grads[1], grads[2], grads[3], grads[4], grads[5], grads[6], grads[7], grads[8], grads[9], grads[10], grads[11], grads[12], grads[13])
```

```python
import functools

import jax
import jax.numpy as jnp
from jax import lax
from jax.experimental import pallas as pl
from jax.experimental.pallas import tpu as pltpu
from jax.sharding import PartitionSpec as P

HEADS = 12
HEAD_DIM = 64
EPSILON = 1e-05
NEGATIVE = -1e30
BF = jnp.bfloat16
F32 = jnp.float32


def dot(a, b, ca, cb):
    return lax.dot_general(a, b, (((ca,), (cb,)), ((), ())), preferred_element_type=F32)


def norm_stats(rows):
    centered = rows - jnp.mean(rows, axis=-1, keepdims=True)
    rstd = lax.rsqrt(jnp.mean(centered * centered, axis=-1, keepdims=True) + EPSILON)
    return centered * rstd, rstd


def norm_back(grad, hat, rstd, gain):
    e = grad * gain
    return rstd * (
        e - jnp.mean(e, axis=-1, keepdims=True) - hat * jnp.mean(e * hat, axis=-1, keepdims=True)
    )


def offsets(length, mine):
    place = lax.broadcasted_iota(jnp.int32, length, 0 if length[1] == 1 else 1)
    group = (place >> 5) & 3
    source = (((group & 1) << 1) | (group >> 1)) ^ mine
    return (place & ~127) | (source << 5) | (place & 31)


def load_blocks(spans, recv, slots, pieces):
    for slot in range(slots):
        where = pl.multiple_of(spans[slot] * 128, 128)
        for row, plain, flipped, factor in pieces:
            block = recv[slot // 2, row : row + 64, (slot % 2) * 128 : (slot % 2) * 128 + 128]
            if factor is not None:
                block = block * jnp.asarray(factor, block.dtype)
            if plain is not None:
                plain[:, pl.ds(where, 128)] = block
            if flipped is not None:
                flipped[pl.ds(where, 128), :] = jnp.transpose(block, (1, 0))


def source_of(group, mine):
    return (((group & 1) << 1) | (group >> 1)) ^ mine


def each_tile(count, tile, body):
    if count <= 4:
        for q in range(count):
            for k in range(q + 1):
                body(q, k, q * tile, k * tile, k == q)
    else:
        def outer(q, _):
            def inner(k, _):
                body(q, k, pl.multiple_of(q * tile, tile), pl.multiple_of(k * tile, tile), False)
                return 0

            lax.fori_loop(0, q, inner, 0)
            body(q, q, pl.multiple_of(q * tile, tile), pl.multiple_of(q * tile, tile), True)
            return 0

        lax.fori_loop(0, count, outer, 0)


TILE = 512


def attend_kernel(spans, mine_ref, recv, out, kept, q_s, kt_s, v_s, m_s, l_s, acc, o_s):
    slots = spans.shape[0]
    total = slots * 128
    mine = mine_ref[0]
    load_blocks(
        spans, recv, slots, ((0, None, q_s, 0.125), (64, kt_s, None, None), (128, None, v_s, None))
    )
    m_s[...] = jnp.full_like(m_s, NEGATIVE)
    l_s[...] = jnp.zeros_like(l_s)
    acc[...] = jnp.zeros_like(acc)

    def body(_q, _k, q0, k0, diagonal):
        rows, cols = pl.ds(q0, TILE), pl.ds(k0, TILE)
        s = jnp.dot(q_s[rows, :], kt_s[:, cols], preferred_element_type=F32)
        if diagonal:
            keep = offsets((TILE, 1), mine) >= offsets((1, TILE), mine)
            s = jnp.where(keep, s, NEGATIVE)
        old = m_s[rows, :]
        new = jnp.maximum(old, jnp.max(s, axis=-1, keepdims=True))
        p = jnp.exp(s - new)
        scale = jnp.exp(old - new)
        l_s[rows, :] = l_s[rows, :] * scale + jnp.sum(p, axis=-1, keepdims=True)
        acc[rows, :] = acc[rows, :] * scale + jnp.dot(
            p.astype(BF), v_s[cols, :], preferred_element_type=F32
        )
        m_s[rows, :] = new

    each_tile(total // TILE, TILE, body)
    o = acc[...] / l_s[...]
    o_s[...] = o.astype(BF)
    kept[:, :64] = o
    kept[:, 64:] = jnp.broadcast_to(m_s[...] + jnp.log(l_s[...]), (total, 64))
    for slot in range(slots):
        for group in range(4):
            where = pl.multiple_of(spans[slot] * 128 + group * 32, 32)
            half = (slot % 2) * 64
            out[slot // 2, source_of(group, mine), :, half : half + 64] = o_s[pl.ds(where, 32), :]


def attend_back_kernel(
    spans, mine_ref, recv, head_grad, kept, out,
    q_s, qt_s, kt_s, k_s, vt_s, do_s, dot_s, delta_s, dq_s, dkt_s, dvt_s,
):
    slots = spans.shape[0]
    total = slots * 128
    mine = mine_ref[0]
    load_blocks(
        spans, recv, slots,
        ((0, qt_s, q_s, 0.125), (64, kt_s, k_s, None), (128, vt_s, None, None)),
    )
    for slot in range(slots):
        for group in range(4):
            where = pl.multiple_of(spans[slot] * 128 + group * 32, 32)
            half = (slot % 2) * 64
            do_s[pl.ds(where, 32), :] = head_grad[
                slot // 2, source_of(group, mine), :, half : half + 64
            ]
    d_out = do_s[...].astype(F32)
    delta_s[...] = jnp.sum(d_out * kept[:, :64], axis=-1, keepdims=True)
    dot_s[...] = jnp.transpose(d_out, (1, 0)).astype(BF)
    dq_s[...] = jnp.zeros_like(dq_s)
    dkt_s[...] = jnp.zeros_like(dkt_s)
    dvt_s[...] = jnp.zeros_like(dvt_s)

    def body(_q, _k, q0, k0, diagonal):
        rows, cols = pl.ds(q0, TILE), pl.ds(k0, TILE)
        s = jnp.dot(q_s[rows, :], kt_s[:, cols], preferred_element_type=F32)
        p = jnp.exp(s - kept[rows, 64:65])
        if diagonal:
            keep = offsets((TILE, 1), mine) >= offsets((1, TILE), mine)
            p = jnp.where(keep, p, 0.0)
        dvt_s[:, cols] += jnp.dot(dot_s[:, rows], p.astype(BF), preferred_element_type=F32)
        dp = jnp.dot(do_s[rows, :], vt_s[:, cols], preferred_element_type=F32)
        ds = (p * (dp - delta_s[rows, :])).astype(BF)
        dkt_s[:, cols] += jnp.dot(qt_s[:, rows], ds, preferred_element_type=F32)
        dq_s[rows, :] += jnp.dot(ds, k_s[cols, :], preferred_element_type=F32)

    each_tile(total // TILE, TILE, body)
    for slot in range(slots):
        where = pl.multiple_of(spans[slot] * 128, 128)
        lanes = slice((slot % 2) * 128, (slot % 2) * 128 + 128)
        dq = dq_s[pl.ds(where, 128), :] * 0.125
        out[slot // 2, 0:64, lanes] = jnp.transpose(dq, (1, 0)).astype(BF)
        out[slot // 2, 64:128, lanes] = dkt_s[:, pl.ds(where, 128)].astype(BF)
        out[slot // 2, 128:192, lanes] = dvt_s[:, pl.ds(where, 128)].astype(BF)


SMEM = pl.BlockSpec(memory_space=pltpu.SMEM)
VMEM = pl.BlockSpec(memory_space=pltpu.VMEM)
BIG = pltpu.CompilerParams(vmem_limit_bytes=60 * 1024 * 1024)


def attend(spans, mine, recv):
    slots = spans.shape[0]
    total = slots * 128
    return pl.pallas_call(
        attend_kernel,
        out_shape=(
            jax.ShapeDtypeStruct((slots // 2, 4, 32, 128), BF),
            jax.ShapeDtypeStruct((total, 128), F32),
        ),
        in_specs=[SMEM, SMEM, VMEM],
        out_specs=(VMEM, VMEM),
        scratch_shapes=[
            pltpu.VMEM((total, 64), BF),
            pltpu.VMEM((64, total), BF),
            pltpu.VMEM((total, 64), BF),
            pltpu.VMEM((total, 1), F32),
            pltpu.VMEM((total, 1), F32),
            pltpu.VMEM((total, 64), F32),
            pltpu.VMEM((total, 64), BF),
        ],
        compiler_params=BIG,
        name="attend",
    )(spans, mine, recv)


def attend_back(spans, mine, recv, head_grad, kept):
    slots = spans.shape[0]
    total = slots * 128
    return pl.pallas_call(
        attend_back_kernel,
        out_shape=jax.ShapeDtypeStruct((slots // 2, 192, 256), BF),
        in_specs=[SMEM, SMEM, VMEM, VMEM, VMEM],
        out_specs=VMEM,
        scratch_shapes=[
            pltpu.VMEM((total, 64), BF),
            pltpu.VMEM((64, total), BF),
            pltpu.VMEM((64, total), BF),
            pltpu.VMEM((total, 64), BF),
            pltpu.VMEM((64, total), BF),
            pltpu.VMEM((total, 64), BF),
            pltpu.VMEM((64, total), BF),
            pltpu.VMEM((total, 1), F32),
            pltpu.VMEM((total, 64), F32),
            pltpu.VMEM((64, total), F32),
            pltpu.VMEM((64, total), F32),
        ],
        compiler_params=BIG,
        name="attend_back",
    )(spans, mine, recv, head_grad, kept)


def swap(value, bit):
    return lax.ppermute(value, "seq", [(i, i ^ bit) for i in range(4)])


def gather_seq(value, axis):
    pair = jnp.concatenate([value, swap(value, 2)], axis=axis)
    return jnp.concatenate([pair, swap(pair, 1)], axis=axis)


def scatter_seq(parts):
    mine = parts[:2] + swap(parts[2:].astype(BF), 1).astype(F32)
    return mine[0] + swap(mine[1].astype(BF), 2).astype(F32)


def gelu(u):
    return jax.nn.gelu(u, approximate=True)


def shards(
    tokens, cotangent, span_order, ln1_gain, ln1_bias, w_qkv, bias_query, bias_value, w_out,
    bias_out, ln2_gain, ln2_bias, w_fc, bias_fc, w_proj, bias_proj,
):
    seqs, slots, rows, width = tokens.shape
    fsdp = lax.axis_size("fsdp")
    group = lax.axis_size("seq")
    mine = lax.axis_index("seq")
    place = lax.axis_index("fsdp")
    heads = HEADS // group
    pairs = seqs * heads
    own = seqs * slots * rows
    shard = width // fsdp
    hidden = w_fc.shape[1]
    part = hidden // group

    quarter_qkv = lax.dynamic_index_in_dim(
        w_qkv.reshape(shard, 3, group, heads, HEAD_DIM), mine, 2, keepdims=False
    )
    quarter_qkv = quarter_qkv.transpose(0, 2, 1, 3).reshape(shard, 3 * heads * HEAD_DIM)
    own_bias_fc = lax.dynamic_index_in_dim(bias_fc.reshape(group, shard), mine, 0, keepdims=False)
    small = jnp.stack(
        [ln1_gain, ln1_bias, bias_query, bias_value, bias_out, ln2_gain, ln2_bias, bias_proj,
         own_bias_fc],
        axis=1,
    )
    packed = jnp.concatenate([quarter_qkv, jnp.pad(small, ((0, 0), (0, 64 - 9)))], axis=1)
    quarter_fc = lax.dynamic_index_in_dim(
        w_fc.reshape(shard, fsdp, group, shard), mine, 2, keepdims=False
    ).reshape(shard, part)
    quarter_proj = lax.dynamic_index_in_dim(
        w_proj.reshape(group, shard, width), mine, 0, keepdims=False
    )

    first = lax.all_to_all(
        jnp.broadcast_to(packed[None], (fsdp,) + packed.shape), "fsdp", 0, 0, tiled=True
    ).reshape(width, packed.shape[1])
    full_out, quarter_fc, quarter_proj, first = lax.optimization_barrier(
        (w_out, quarter_fc, quarter_proj, first)
    )
    full_out = lax.all_gather(full_out, "fsdp", axis=0, tiled=True)
    full_fc = lax.all_gather(quarter_fc, "fsdp", axis=0, tiled=True)
    full_proj = lax.all_gather(quarter_proj, "fsdp", axis=0, tiled=True)
    weight = first[:, : 3 * heads * HEAD_DIM]
    vectors = jnp.transpose(first[:, 3 * heads * HEAD_DIM :][:, :9], (1, 0)).astype(F32)
    gain_one, offset_one, bias_q, bias_v, bias_o, gain_two, offset_two, bias_p, bias_f = (
        vectors[i] for i in range(9)
    )

    x = tokens.reshape(own, width).astype(F32)
    hat_one, rstd_one = norm_stats(x)
    normed_one = (hat_one * gain_one + offset_one).astype(BF)
    wide_one = gather_seq(normed_one.reshape(seqs, slots, 1, rows, width), 2)
    wide_one = wide_one.reshape(group * own, width)
    upstream = cotangent.reshape(own, width)
    wide_up = gather_seq(upstream, 0)

    bias_rows = jnp.stack(
        [
            lax.dynamic_slice_in_dim(bias_q, mine * heads * HEAD_DIM, heads * HEAD_DIM),
            jnp.zeros((heads * HEAD_DIM,), F32),
            lax.dynamic_slice_in_dim(bias_v, mine * heads * HEAD_DIM, heads * HEAD_DIM),
        ]
    )
    bias_rows = bias_rows.reshape(3, heads, HEAD_DIM).transpose(1, 0, 2).reshape(-1, 1)
    features = (dot(weight, wide_one, 0, 1) + bias_rows).astype(BF)
    per_seq = slots * group * rows
    outgoing = features.reshape(heads, 3 * HEAD_DIM, seqs, per_seq).transpose(2, 0, 1, 3)
    outgoing = outgoing.reshape(pairs, 3 * HEAD_DIM, per_seq)
    outgoing = jnp.pad(outgoing, ((0, fsdp - pairs), (0, 0), (0, 0)))
    recv = lax.all_to_all(outgoing, "fsdp", 0, 0, tiled=True)

    my_seq = jnp.minimum(place // heads, seqs - 1)
    spans = lax.dynamic_index_in_dim(span_order, my_seq, 0, keepdims=False)
    mine_array = mine.reshape(1).astype(jnp.int32)
    attn_out, kept = attend(spans, mine_array, recv)
    home = lax.all_to_all(
        attn_out.reshape(fsdp * group, rows, slots * HEAD_DIM), ("fsdp", "seq"), 0, 0, tiled=True
    )
    home = home.reshape(fsdp, group, rows, slots, HEAD_DIM)[:pairs]
    attn = home.reshape(seqs, heads, group, rows, slots, HEAD_DIM).transpose(0, 4, 3, 2, 1, 5)
    attn = attn.reshape(own, width)

    residual = x + dot(attn, full_out, 1, 0) + bias_o
    hat_two, rstd_two = norm_stats(residual)
    normed_two = (hat_two * gain_two + offset_two).astype(BF)
    wide_two = gather_seq(normed_two, 0)

    pre = dot(wide_two, full_fc, 1, 0) + bias_f
    act_grad = dot(wide_up, full_proj, 1, 1)
    act, back = jax.vjp(gelu, pre)
    d_pre = back(act_grad)[0].astype(BF)
    act = act.astype(BF)
    d_norm2 = scatter_seq(dot(d_pre, full_fc, 1, 1).reshape(group, own, width))
    layer_out = residual + bias_p + scatter_seq(
        dot(act, full_proj, 1, 0).reshape(group, own, width)
    )

    d_residual = upstream.astype(F32) + norm_back(d_norm2, hat_two, rstd_two, gain_two)
    d_y = d_residual.astype(BF)
    d_attn = dot(d_y, full_out, 1, 1).astype(BF)
    to_heads = d_attn.reshape(seqs, slots, rows, group, heads, HEAD_DIM).transpose(0, 4, 3, 2, 1, 5)
    to_heads = to_heads.reshape(pairs, group, rows, slots * HEAD_DIM)
    to_heads = jnp.pad(to_heads, ((0, fsdp - pairs), (0, 0), (0, 0), (0, 0)))
    head_grad = lax.all_to_all(
        to_heads.reshape(fsdp * group, rows, slots * HEAD_DIM), ("fsdp", "seq"), 0, 0, tiled=True
    ).reshape(fsdp, group, rows, slots * HEAD_DIM)

    grad_proj = dot(act, wide_up, 0, 0).astype(BF)
    grad_fc = dot(wide_two, d_pre, 0, 0).astype(BF)
    grad_out = dot(attn, d_y, 0, 0).astype(BF)
    share_proj = lax.psum_scatter(grad_proj, "fsdp", scatter_dimension=0, tiled=True)
    share_fc = lax.psum_scatter(grad_fc, "fsdp", scatter_dimension=0, tiled=True)
    share_out = lax.psum_scatter(grad_out, "fsdp", scatter_dimension=0, tiled=True)

    d_features = attend_back(spans, mine_array, recv, head_grad, kept)
    d_features = lax.all_to_all(d_features, "fsdp", 0, 0, tiled=True)[:pairs]
    d_features = d_features.reshape(seqs, heads, 3 * HEAD_DIM, per_seq).transpose(1, 2, 0, 3)
    d_features = d_features.reshape(heads * 3 * HEAD_DIM, seqs * per_seq)
    grad_qkv = dot(wide_one, d_features, 0, 1).astype(BF)
    share_qkv = lax.all_to_all(grad_qkv.reshape(fsdp, shard, -1), "fsdp", 0, 0, tiled=True)
    share_qkv = jnp.sum(share_qkv.astype(F32), axis=0).astype(BF)
    wide_back = dot(d_features, weight, 0, 1)
    wide_back = wide_back.reshape(seqs, slots, group, rows, width).transpose(2, 0, 1, 3, 4)
    d_norm1 = scatter_seq(wide_back.reshape(group, own, width))
    input_grad = d_residual + norm_back(d_norm1, hat_one, rstd_one, gain_one)

    d_cols = jnp.sum(d_features.astype(F32), axis=1).reshape(heads, 3, HEAD_DIM)

    def placed_columns(values):
        return lax.dynamic_update_slice_in_dim(
            jnp.zeros((width,), F32), values.reshape(-1), mine * heads * HEAD_DIM, 0
        )

    vectors = jnp.stack(
        [
            jnp.sum(d_norm1 * hat_one, axis=0),
            jnp.sum(d_norm1, axis=0),
            placed_columns(d_cols[:, 0]),
            placed_columns(d_cols[:, 2]),
            jnp.sum(d_y.astype(F32), axis=0),
            jnp.sum(d_norm2 * hat_two, axis=0),
            jnp.sum(d_norm2, axis=0),
            jnp.sum(upstream.astype(F32), axis=0),
        ]
    ).reshape(8, fsdp, shard)
    columns_fc = jnp.sum(d_pre.astype(F32), axis=0).reshape(1, fsdp, shard)
    columns_fc = lax.dynamic_update_slice_in_dim(
        jnp.zeros((group, fsdp, shard), F32), columns_fc, mine, 0
    )
    small = jnp.concatenate([vectors, columns_fc], axis=0).transpose(1, 0, 2).reshape(fsdp, -1)
    small = jnp.broadcast_to(small.astype(BF)[:, None], (fsdp, group, small.shape[1]))
    small = lax.all_to_all(
        small.reshape(fsdp * group, -1), ("fsdp", "seq"), 0, 0, tiled=True
    )
    small = jnp.sum(small.astype(F32), axis=0).reshape(8 + group, shard)

    shares = jnp.concatenate([share_proj, share_fc, share_out], axis=0)
    shares = gather_seq(shares[None], 0)
    wide_qkv = gather_seq(share_qkv[None], 0)

    def absolute(index):
        source = index ^ mine
        return ((source & 1) << 1) | (source >> 1)

    ordered = jnp.stack(
        [lax.dynamic_index_in_dim(shares, absolute(i), 0, keepdims=False) for i in range(group)]
    ).astype(F32)
    full_proj_grad = ordered[:, :shard].reshape(group * shard, width)
    full_fc_grad = ordered[:, shard : 2 * shard].reshape(group, shard, fsdp, shard)
    full_fc_grad = full_fc_grad.transpose(1, 2, 0, 3).reshape(shard, hidden)
    full_out_grad = jnp.sum(ordered[:, 2 * shard :], axis=0)
    ordered_qkv = jnp.stack(
        [lax.dynamic_index_in_dim(wide_qkv, absolute(i), 0, keepdims=False) for i in range(group)]
    ).astype(F32)
    full_qkv_grad = ordered_qkv.reshape(group, shard, heads, 3, HEAD_DIM).transpose(1, 3, 0, 2, 4)
    full_qkv_grad = full_qkv_grad.reshape(shard, 3 * width)
    return (
        layer_out.reshape(tokens.shape),
        input_grad.reshape(tokens.shape),
        small[0],
        small[1],
        full_qkv_grad,
        small[2],
        small[3],
        full_out_grad,
        small[4],
        small[5],
        small[6],
        full_fc_grad,
        small[8:].reshape(-1),
        full_proj_grad,
        small[7],
    )


def solution(mesh):
    rows = P(None, "fsdp", "seq", None)
    vector, matrix = P("fsdp"), P("fsdp", None)
    return jax.shard_map(
        shards,
        mesh=mesh,
        in_specs=(
            rows, rows, P(), vector, vector, matrix, vector, vector, matrix, vector, vector, vector,
            matrix, vector, matrix, vector,
        ),
        out_specs=(
            rows, rows, vector, vector, matrix, vector, vector, matrix, vector, vector, vector,
            matrix, vector, matrix, vector,
        ),
        check_vma=False,
    )
```
